32 devices in a mesh: groups: 2 (over x), shard: 16 (over z, y, core).
Axes of the slice: x: 2, y: 2, z: 4, core: 2. Of those that a mesh axis runs over, the one named last changes fastest.
Arguments:
- hidden: bfloat16 [8192, 2048], P(('groups', 'shard')), parts along dimension 0, may hold values from -10 to 10
- query_rows: bfloat16 [8192, 4096], P(('groups', 'shard')), parts along dimension 0, may hold values from -9 to 9
- key_rows: bfloat16 [8192, 512], P(('groups', 'shard')), parts along dimension 0, may hold values from -9 to 9
- value_rows: bfloat16 [8192, 512], P(('groups', 'shard')), parts along dimension 0, may hold values from -6 to 6
- counts: int32 [2], P('groups'), parts along dimension 0, may hold values from 1024 to 4096
- out_weight: bfloat16 [4096, 2048], P('shard'), may hold values from -0.09375 to 0.09375
- norm_gain: bfloat16 [2048], replicated, may hold values from 0.099609375 to 1.8984375
- route_ids: int32 [8192, 8], P(('groups', 'shard')), parts along dimension 0, may hold values from 0 to 31, all different within a row; in each aligned block of 256 rows (0 to 255, 256 to 511, ...) at most 80 rows name the same one
- route_weights: bfloat16 [8192, 8], P(('groups', 'shard')), parts along dimension 0, may hold values from 0.099609375 to 0.3984375
- w_gate: bfloat16 [32, 2048, 768], P('shard'), may hold values from -0.125 to 0.125
- w_up: bfloat16 [32, 2048, 768], P('shard'), may hold values from -0.125 to 0.125
- w_down: bfloat16 [32, 768, 2048], P('shard'), may hold values from -0.21875 to 0.21875
Outputs:
- layer_out: bfloat16 [8192, 2048], P(('groups', 'shard')), parts along dimension 0
The draws below stay inside these ranges and needn't reach their ends.
There are 2 independent parts, one for each index of `groups`. The reference program is written for one: setup_inputs(seed, part) draws one part's arguments, and reference() takes and returns one part's arrays. A program takes and returns all parts, laid end to end along the dimension named above; an argument that names none is the same for every part. Nothing has to cross between parts.
Inputs may be any that keep to these rules, and one draw needn't show every extreme that they name: `route_ids`: each row names 8 different experts; in the rows of one device no expert is named by more than 80 rows, a bound that some block reaches.
All inputs are finite; a program needn't handle non-finite values.
Results may differ from the reference program's by a relative error of at most 0.008.
Values may be sent and summed in bfloat16 or wider, within the bound.
A program may use at most 384 MiB of HBM per device.

```python
import math
import jax
import jax.numpy as jnp
import numpy as np
from jax import lax

D = 2048
HEADS = 32
KV_HEADS = 4
HD = 128
FF = 768
TOPK = 8
SEQS = 1
SEQ_LEN = 4096
EXPERTS = 32
TOKENS = 4096
TOK_DEV = 256
CAP = 80
N_SHARD = 16


def draw_query_rows(key, part):
    result = jnp.clip(jax.random.normal(jax.random.fold_in(key, 1), (TOKENS, HEADS, HD), jnp.float32), -5.0, 5.0)
    return result.reshape(TOKENS, HEADS * HD).astype(jnp.bfloat16)


def draw_key_rows(key, part):
    result = jnp.clip(jax.random.normal(jax.random.fold_in(key, 2), (TOKENS, KV_HEADS, HD), jnp.float32), -5.0, 5.0)
    return result.reshape(TOKENS, KV_HEADS * HD).astype(jnp.bfloat16)


def draw_hidden(key, part):
    result = jnp.clip(jax.random.normal(jax.random.fold_in(key, 3), (TOKENS, D), jnp.float32), -5.0, 5.0)
    return result.astype(jnp.bfloat16)


def block_scale(rng, dims, shards, least, top_value):
    gain = 1.0
    for axis_at, shards_of in shards:
        heights = jax.random.uniform(jax.random.fold_in(jax.random.fold_in(rng, 6), axis_at), (shards_of,), jnp.float32, least / len(shards), top_value / len(shards))
        gain = gain * jnp.repeat(jnp.exp(heights), dims[axis_at] // shards_of).reshape((-1,) + (1,) * (len(dims) - 1 - axis_at))
    return gain


def shared_out(stream_key, own, number, rows, count, top, most, slope):
    sequence = jax.random.permutation(stream_key, count)
    heavy_load, usual = load_shares(count, rows * top, most, slope, True), load_shares(count, rows * top, most, slope, False)
    places = jnp.arange(count)

    def named(sizes, rotation):
        used = int((sizes > 0).sum())
        fixed = max(1, used // 4)
        shifted = fixed + (places - fixed + rotation * (used - fixed)) % max(1, count - fixed)
        return jnp.zeros((count,), jnp.int32).at[sequence[jnp.where(places < fixed, places, shifted)]].set(jnp.asarray(sizes, jnp.int32))

    sizes = jnp.where(number % 4 == 0, named(heavy_load, number // 4), named(usual, number - number // 4 - 1))
    mixed = jax.random.permutation(jax.random.fold_in(own, 3), count)
    giver, receiver = mixed[0:count // 2 * 2:2], mixed[1:count // 2 * 2:2]
    margin = jnp.minimum(sizes[giver] - 1, most - sizes[receiver]) // 2
    margin = jnp.where((giver == sequence[0]) | (receiver == sequence[0]) | (sizes[receiver] == 0), 0, jnp.maximum(margin, 0))
    shifted = jax.random.randint(jax.random.fold_in(own, 4), (count // 2,), 0, 1 << 20) % (margin + 1)
    sizes = sizes.at[giver].add(-shifted).at[receiver].add(shifted)
    members = jnp.searchsorted(jnp.cumsum(sizes), jnp.arange(rows * top), side="right").astype(jnp.int32)
    listing = members.reshape(top, rows).T
    listing = listing[jax.random.permutation(jax.random.fold_in(own, 1), rows)]
    rotation = jax.random.randint(jax.random.fold_in(own, 2), (rows, 1), 0, top)
    return jnp.take_along_axis(listing, (jnp.arange(top)[None, :] + rotation) % top, axis=1)


def load_shares(amount, total, reach, slope, full):
    portions = [(1 << 20) // math.isqrt(rank ** slope) + 1 for rank in range(1, amount + 1)]
    largest = reach if full else min(reach, max(-(-total // amount), total * portions[0] // sum(portions)))
    least = 1 if total - largest >= amount - 1 else 0
    given, surplus = [largest] + [least] * (amount - 1), total - largest - least * (amount - 1)
    while surplus > 0:
        free = [i for i in range(1, amount) if given[i] < largest] or [i for i in range(1, amount) if given[i] < reach]
        mass, budget = sum([portions[i] for i in free]), surplus
        for i in free:
            extra = min(reach - given[i], max(1, budget * portions[i] // mass), surplus)
            given[i] = given[i] + extra
            surplus = surplus - extra
    return np.array(given)


def normal_values(key, dims, width, reach, cuts=(), kind=jnp.bfloat16):
    values = jax.random.normal(key, dims, jnp.float32) * width
    if len(cuts) > 0:
        values = block_scale(key, dims, cuts, -0.22, 0.18) * values
    return jnp.clip(values, min=-reach, max=reach).astype(kind)


def setup_inputs(seed: int = 0, part: int = 0) -> dict:
    streams_of = jax.random.split(jax.random.key(seed), 13)
    part_splits = jax.random.split(jax.random.fold_in(streams_of[12], part), 13)
    hidden = draw_hidden(jax.random.fold_in(jax.random.fold_in(streams_of[12], part), 71), part)
    query_rows = draw_query_rows(jax.random.fold_in(jax.random.fold_in(streams_of[12], part), 71), part)
    key_rows = draw_key_rows(jax.random.fold_in(jax.random.fold_in(streams_of[12], part), 71), part)
    value_rows = normal_values(part_splits[3], (TOKENS, KV_HEADS * HD), 1.0, 6.0, ((0, 16),))
    counts = jax.random.randint(part_splits[4], (SEQS,), SEQ_LEN // 4, SEQ_LEN + 1).astype(jnp.int32)
    out_weight = normal_values(streams_of[5], (HEADS * HD, D), (HEADS * HD) ** -0.5, 0.09375, ((0, 16),))
    norm_gain = jnp.clip(1.0 + 0.18 * jax.random.normal(streams_of[6], (D,), jnp.float32), 0.099609375, 1.8984375).astype(jnp.bfloat16)
    route_ids_keys = jax.random.split(jax.random.fold_in(part_splits[7], 1), TOKENS // TOK_DEV)
    route_ids_turns = jax.random.permutation(jax.random.fold_in(part_splits[7], 3), TOKENS // TOK_DEV)
    route_ids = jax.vmap(lambda own, number: shared_out(jax.random.fold_in(part_splits[7], 2), own, number, TOK_DEV, EXPERTS, TOPK, CAP, 2))(route_ids_keys, route_ids_turns).reshape((TOKENS, TOPK))
    route_weights = jnp.clip(0.099609375 + 0.29882812 * jax.random.uniform(part_splits[8], (TOKENS, TOPK), jnp.float32) ** block_scale(part_splits[8], (TOKENS, TOPK), ((0, 16),), -0.2, 0.2), 0.099609375, 0.3984375).astype(jnp.bfloat16)
    w_gate = normal_values(streams_of[9], (EXPERTS, D, FF), D ** -0.5, 0.125, ((0, 16),))
    w_up = normal_values(streams_of[10], (EXPERTS, D, FF), D ** -0.5, 0.125, ((0, 16),))
    w_down = normal_values(streams_of[11], (EXPERTS, FF, D), FF ** -0.5, 0.21875, ((0, 16),))
    return dict(hidden=hidden, query_rows=query_rows, key_rows=key_rows, value_rows=value_rows, counts=counts, out_weight=out_weight, norm_gain=norm_gain, route_ids=route_ids, route_weights=route_weights, w_gate=w_gate, w_up=w_up, w_down=w_down)


def attend_sequence(query_seq, key_seq, value_seq, live_count):
    length = query_seq.shape[0]
    group_size = HEADS // KV_HEADS
    score_scale = 1.0 / HD ** 0.5
    row_pos = jnp.arange(length)[:, None]
    col_pos = jnp.arange(length)[None, :]
    visible = (col_pos <= row_pos) & (col_pos < live_count)
    live_rows = jnp.arange(length) < live_count
    query_heads = query_seq.reshape(length, HEADS, HD).transpose(1, 0, 2)
    key_heads = key_seq.reshape(length, KV_HEADS, HD).transpose(1, 0, 2)
    value_heads = value_seq.reshape(length, KV_HEADS, HD).transpose(1, 0, 2)

    def one_head(head_index):
        query_here = query_heads[head_index]
        key_here = key_heads[head_index // group_size]
        value_here = value_heads[head_index // group_size]
        scores = jnp.dot(query_here, key_here.T, preferred_element_type=jnp.float32) * score_scale
        row_max = lax.optimization_barrier(jnp.max(jnp.where(visible, scores, -1e+30), axis=1, keepdims=True))
        expo = jnp.where(visible, jnp.exp(scores - row_max), 0.0)
        denom = lax.optimization_barrier(jnp.sum(expo, axis=1, keepdims=True))
        summed = jnp.dot(expo.astype(jnp.bfloat16), value_here, preferred_element_type=jnp.float32)
        result = jnp.where(live_rows[:, None], summed / denom, 0.0)
        return result.astype(jnp.bfloat16)
    outputs = lax.map(one_head, jnp.arange(HEADS))
    return outputs.transpose(1, 0, 2).reshape(length, HEADS * HD)

def reference(hidden, query_rows, key_rows, value_rows, counts, out_weight, norm_gain, route_ids, route_weights, w_gate, w_up, w_down):
    pieces = []
    for seq_number in range(SEQS):
        row_start = seq_number * SEQ_LEN
        pieces.append(attend_sequence(query_rows[row_start:row_start + SEQ_LEN], key_rows[row_start:row_start + SEQ_LEN], value_rows[row_start:row_start + SEQ_LEN], counts[seq_number]))
    attended = jnp.concatenate(pieces, axis=0)
    group_cols = HEADS // N_SHARD * HD

    def add_group(total, group_index):
        col_start = (group_index * group_cols).astype(jnp.int32)
        cols = lax.dynamic_slice_in_dim(attended, col_start, group_cols, 1)
        rows = lax.dynamic_slice_in_dim(out_weight, col_start, group_cols, 0)
        part = jnp.dot(cols, rows, preferred_element_type=jnp.float32).astype(jnp.bfloat16)
        part = lax.optimization_barrier(part)
        return (total + part.astype(jnp.float32), None)
    head_total, _ = lax.scan(add_group, jnp.zeros((TOKENS, D), jnp.float32), jnp.arange(N_SHARD, dtype=jnp.int32))
    mixed_rows = hidden.astype(jnp.float32) + head_total
    mean_square = lax.optimization_barrier(jnp.mean(mixed_rows * mixed_rows, axis=1, keepdims=True))
    normed = (mixed_rows * lax.rsqrt(mean_square + 1e-06) * norm_gain.astype(jnp.float32)).astype(jnp.bfloat16)
    token_index = jnp.arange(TOKENS)
    token_live = token_index % SEQ_LEN < counts[token_index // SEQ_LEN]
    route_live = jnp.where(token_live[:, None], route_weights.astype(jnp.float32), jnp.float32(0.0))
    limit = N_SHARD * CAP

    def expert_step(expert_sum, expert):
        matches = route_ids == expert
        weight_row = lax.optimization_barrier(jnp.sum(jnp.where(matches, route_live, jnp.float32(0.0)), axis=1))
        hit_row = jnp.any(matches, axis=1)
        chosen = jnp.nonzero(hit_row, size=limit, fill_value=0)[0]
        valid = jnp.arange(limit) < jnp.sum(hit_row.astype(jnp.int32))
        chosen_rows = normed[chosen]
        gate_proj = jnp.dot(chosen_rows, w_gate[expert], preferred_element_type=jnp.float32)
        up_proj = jnp.dot(chosen_rows, w_up[expert], preferred_element_type=jnp.float32)
        activated = (jax.nn.silu(gate_proj) * up_proj).astype(jnp.bfloat16)
        output = jnp.dot(activated, w_down[expert], preferred_element_type=jnp.float32)
        contribution = (weight_row[chosen][:, None] * output).astype(jnp.bfloat16)
        contribution = lax.optimization_barrier(contribution).astype(jnp.float32)
        contribution = jnp.where(valid[:, None], contribution, jnp.float32(0.0))
        return (expert_sum.at[chosen].add(contribution), None)
    expert_sum, _ = lax.scan(expert_step, jnp.zeros((TOKENS, D), jnp.float32), jnp.arange(EXPERTS))
    return (mixed_rows + expert_sum).astype(jnp.bfloat16)
```

```python
import functools
import math

import jax
import jax.numpy as jnp
from jax import lax
from jax.experimental import pallas as pl
from jax.experimental.pallas import tpu as pltpu
from jax.sharding import PartitionSpec as P

HD = 128
SEQ_LEN = 4096
NEG = -1e30
MESH = pl.DeviceIdType.MESH


def ring_place(chips, index):
    if chips == 8:
        z, y = index // 2, index % 2
        return z + y * (7 - 2 * z)
    return index


def ring_chip(chips, place):
    if chips == 8:
        half = place // 4
        z = place + half * (7 - 2 * place)
        return 2 * z + half
    return place


def gather_kernel(devices, pieces, x_ref, o_ref, local_sem, near_send, near_recv, send, recv):
    chips = devices // 2
    me = lax.axis_index("shard")
    group = lax.axis_index("groups")
    core = me % 2
    place = ring_place(chips, me // 2)

    def device_at(offset):
        return ring_chip(chips, (place + offset + 2 * chips) % chips) * 2 + core

    right, left, sibling = device_at(1), device_at(-1), me + 1 - 2 * core
    barrier = pltpu.get_barrier_semaphore()
    for other in (right, left, sibling):
        pl.semaphore_signal(barrier, inc=1, device_id=(group, other), device_id_type=MESH)
    pl.semaphore_wait(barrier, 3)

    rows = x_ref.shape[0] // (2 * pieces)

    def part(ref, way, piece):
        return ref.at[pl.ds((way * pieces + piece) * rows, rows)]

    def hop(step, way, piece):
        origin = device_at(-step if way == 0 else step)
        src = part(x_ref if step == 0 else o_ref.at[origin], way, piece)
        return pltpu.make_async_remote_copy(
            src_ref=src,
            dst_ref=part(o_ref.at[origin], way, piece),
            send_sem=send.at[step, way, piece],
            recv_sem=recv.at[step, way, piece],
            device_id=(group, right if way == 0 else left),
            device_id_type=MESH,
        )

    def landing(step, way, piece):
        origin = device_at(-step - 1 if way == 0 else step + 1)
        place_of = part(o_ref.at[origin], way, piece)
        return pltpu.make_async_remote_copy(
            src_ref=place_of,
            dst_ref=place_of,
            send_sem=send.at[step, way, piece],
            recv_sem=recv.at[step, way, piece],
            device_id=(group, right if way == 0 else left),
            device_id_type=MESH,
        )

    def near(step, way, piece):
        if step < 0:
            src, origin = part(x_ref, way, piece), me
        else:
            origin = device_at(-step - 1 if way == 0 else step + 1)
            src = part(o_ref.at[origin], way, piece)
        return pltpu.make_async_remote_copy(
            src_ref=src,
            dst_ref=part(o_ref.at[origin], way, piece),
            send_sem=near_send.at[step + 1, way, piece],
            recv_sem=near_recv.at[step + 1, way, piece],
            device_id=(group, sibling),
            device_id_type=MESH,
        )

    def near_landing(step, way, piece):
        if step < 0:
            origin = sibling
        else:
            origin = device_at(-step - 1 if way == 0 else step + 1) + 1 - 2 * core
        place_of = part(o_ref.at[origin], way, piece)
        return pltpu.make_async_remote_copy(
            src_ref=place_of,
            dst_ref=place_of,
            send_sem=near_send.at[step + 1, way, piece],
            recv_sem=near_recv.at[step + 1, way, piece],
            device_id=(group, sibling),
            device_id_type=MESH,
        )

    every = [(way, piece) for piece in range(pieces) for way in range(2)]
    for way, piece in every:
        hop(0, way, piece).start()
    own = pltpu.make_async_copy(x_ref, o_ref.at[me], local_sem)
    own.start()
    for way, piece in every:
        near(-1, way, piece).start()
    for step in range(chips - 1):
        for way, piece in every:
            landing(step, way, piece).wait_recv()
            if step + 1 < chips - 1:
                hop(step + 1, way, piece).start()
            near(step, way, piece).start()
    own.wait()
    for step in range(chips - 1):
        for way, piece in every:
            hop(step, way, piece).wait_send()
    for step in range(-1, chips - 1):
        for way, piece in every:
            near(step, way, piece).wait_send()
            near_landing(step, way, piece).wait_recv()


def ring_gather(x, devices, collective_id, pieces=2):
    steps = devices // 2
    dma = pltpu.SemaphoreType.DMA
    return pl.pallas_call(
        functools.partial(gather_kernel, devices, pieces),
        out_shape=jax.ShapeDtypeStruct((devices,) + x.shape, x.dtype),
        in_specs=[pl.BlockSpec(memory_space=pltpu.HBM)],
        out_specs=pl.BlockSpec(memory_space=pltpu.HBM),
        scratch_shapes=[
            dma,
            dma((steps, 2, pieces)),
            dma((steps, 2, pieces)),
            dma((steps, 2, pieces)),
            dma((steps, 2, pieces)),
        ],
        compiler_params=pltpu.CompilerParams(collective_id=collective_id, has_side_effects=True),
    )(x)


def attend_kernel(step_rows, heads, count_ref, first_ref, q_ref, k_ref, v_ref, o_ref, qs, top, total):
    rows = q_ref.shape[0]
    scale = math.log2(math.e) / math.sqrt(HD)
    count = count_ref[0]
    first = first_ref[0]
    seen = jnp.minimum(count, first + rows)
    blocks = jnp.where(first < count, (seen + step_rows - 1) // step_rows, 0)
    for h in range(heads):
        qs[h * rows : (h + 1) * rows, :] = q_ref[:, h * HD : (h + 1) * HD]
    top[...] = jnp.full(top.shape, NEG, jnp.float32)
    total[...] = jnp.zeros(total.shape, jnp.float32)
    ones = jnp.ones((step_rows, HD), jnp.bfloat16)

    def fold(start, masked):
        start = pl.multiple_of(start, step_rows)
        keys = k_ref[pl.ds(start, step_rows), :]
        values = jnp.concatenate([v_ref[pl.ds(start, step_rows), :], ones], axis=1)
        if masked:
            at_row = first + lax.broadcasted_iota(jnp.int32, (rows, step_rows), 0)
            at_col = start + lax.broadcasted_iota(jnp.int32, (rows, step_rows), 1)
            visible = (at_col <= at_row) & (at_col < count)
        for h in range(heads):
            span = slice(h * rows, (h + 1) * rows)
            scores = lax.dot_general(
                qs[span, :], keys, (((1,), (1,)), ((), ())), preferred_element_type=jnp.float32
            )
            if masked:
                scores = jnp.where(visible, scores, NEG)
            old = top[span, :]
            new = jnp.maximum(old, jnp.max(scores, axis=1, keepdims=True) * scale)
            expo = jnp.exp2(scores * scale - new[:, :1]).astype(jnp.bfloat16)
            factor = jnp.exp2(old - new)
            part = jnp.dot(expo, values, preferred_element_type=jnp.float32)
            total[span, :] = total[span, :] * jnp.concatenate([factor, factor], axis=1) + part
            top[span, :] = new

    def body(i, carry):
        fold(i * step_rows, False)
        return carry

    lax.fori_loop(0, blocks - 1, body, 0)

    @pl.when(blocks > 0)
    def _():
        fold((blocks - 1) * step_rows, True)

    live = first + lax.broadcasted_iota(jnp.int32, (rows, HD), 0) < count
    for h in range(heads):
        both = total[h * rows : (h + 1) * rows, :]
        result = jnp.where(live, both[:, :HD] / jnp.where(live, both[:, HD:], 1.0), 0.0)
        o_ref[:, h * HD : (h + 1) * HD] = result.astype(jnp.bfloat16)


def attend(count, first, queries, keys_values):
    rows, width = queries.shape
    length, both = keys_values.shape
    kv_count = both // (2 * HD)
    heads = width // HD // kv_count
    step_rows = math.gcd(length, 512)
    smem = pl.BlockSpec(memory_space=pltpu.SMEM)
    return pl.pallas_call(
        functools.partial(attend_kernel, step_rows, heads),
        grid=(kv_count,),
        out_shape=jax.ShapeDtypeStruct((rows, width), jnp.bfloat16),
        in_specs=[
            smem,
            smem,
            pl.BlockSpec((rows, heads * HD), lambda g: (0, g)),
            pl.BlockSpec((length, HD), lambda g: (0, g)),
            pl.BlockSpec((length, HD), lambda g: (0, kv_count + g)),
        ],
        out_specs=pl.BlockSpec((rows, heads * HD), lambda g: (0, g)),
        scratch_shapes=[
            pltpu.VMEM((heads * rows, HD), jnp.bfloat16),
            pltpu.VMEM((heads * rows, HD), jnp.float32),
            pltpu.VMEM((heads * rows, 2 * HD), jnp.float32),
        ],
        compiler_params=pltpu.CompilerParams(vmem_limit_bytes=40 << 20),
        cost_estimate=pl.CostEstimate(
            flops=4 * rows * width * length, bytes_accessed=12 << 20, transcendentals=rows * width * length // HD
        ),
    )(count, first, queries, keys_values, keys_values)


def expert_kernel(local, cap, per, count_ref, x_ref, info_ref, wg_ref, wu_ref, wd_ref, o_ref, picked, given):
    rows = x_ref.shape[1]
    start = pl.program_id(0) * per * rows
    alive = start % SEQ_LEN < count_ref[0]

    @pl.when(jnp.logical_not(alive))
    def _():
        o_ref[...] = jnp.zeros(o_ref.shape, o_ref.dtype)

    @pl.when(alive)
    def _():
        before = (
            lax.broadcasted_iota(jnp.int32, (rows, rows), 0)
            < lax.broadcasted_iota(jnp.int32, (rows, rows), 1)
        ).astype(jnp.bfloat16)
        slot_at = lax.broadcasted_iota(jnp.int32, (cap, rows), 0).astype(jnp.float32)
        choices = []
        weights = [[] for _ in range(local)]
        for b in range(per):
            info = info_ref[b]
            slots = jnp.dot(info.astype(jnp.bfloat16), before, preferred_element_type=jnp.float32)
            mine = []
            for e in range(local):
                hit = (slot_at == slots[e : e + 1]) & (info[e : e + 1] > 0.5)
                mine.append(jnp.where(hit, 1.0, 0.0))
                weights[e].append(
                    jnp.sum(
                        jnp.where(hit, info[local + e : local + e + 1], 0.0), axis=1, keepdims=True
                    )
                )
            choice = jnp.concatenate(mine, axis=0).astype(jnp.bfloat16)
            choices.append(choice)
            rows_here = jnp.dot(choice, x_ref[b], preferred_element_type=jnp.float32)
            rows_here = rows_here.astype(jnp.bfloat16)
            for e in range(local):
                picked[e, b * cap : (b + 1) * cap, :] = rows_here[e * cap : (e + 1) * cap]
        for e in range(local):
            mine = picked[e]
            gate = jnp.dot(mine, wg_ref[e], preferred_element_type=jnp.float32)
            up = jnp.dot(mine, wu_ref[e], preferred_element_type=jnp.float32)
            act = (gate / (1.0 + jnp.exp(-gate)) * up).astype(jnp.bfloat16)
            down = jnp.dot(act, wd_ref[e], preferred_element_type=jnp.float32)
            down = (down * jnp.concatenate(weights[e], axis=0)).astype(jnp.bfloat16)
            for b in range(per):
                given[b, e * cap : (e + 1) * cap, :] = down[b * cap : (b + 1) * cap]
        for b in range(per):
            back = lax.dot_general(
                choices[b], given[b], (((0,), (0,)), ((), ())), preferred_element_type=jnp.float32
            )
            o_ref[b] = back.astype(o_ref.dtype)


def expert_sums(count, rows_all, info, w_gate, w_up, w_down, cap):
    devices, rows, depth = rows_all.shape
    local, _, hidden_units = w_gate.shape
    per = 4
    whole = pl.Buffered(1)
    return pl.pallas_call(
        functools.partial(expert_kernel, local, cap, per),
        grid=(devices // per,),
        out_shape=jax.ShapeDtypeStruct((devices, rows, depth), jnp.bfloat16),
        in_specs=[
            pl.BlockSpec(memory_space=pltpu.SMEM),
            pl.BlockSpec((per, rows, depth), lambda i: (i, 0, 0)),
            pl.BlockSpec((per,) + info.shape[1:], lambda i: (i, 0, 0)),
            pl.BlockSpec(w_gate.shape, lambda i: (0, 0, 0), pipeline_mode=whole),
            pl.BlockSpec(w_up.shape, lambda i: (0, 0, 0), pipeline_mode=whole),
            pl.BlockSpec(w_down.shape, lambda i: (0, 0, 0), pipeline_mode=whole),
        ],
        out_specs=pl.BlockSpec((per, rows, depth), lambda i: (i, 0, 0)),
        scratch_shapes=[
            pltpu.VMEM((local, per * cap, depth), jnp.bfloat16),
            pltpu.VMEM((per, local * cap, depth), jnp.bfloat16),
        ],
        compiler_params=pltpu.CompilerParams(vmem_limit_bytes=60 << 20),
    )(count, rows_all, info, w_gate, w_up, w_down)


def per_device(
    hidden,
    query_rows,
    key_rows,
    value_rows,
    counts,
    out_weight,
    norm_gain,
    route_ids,
    route_weights,
    w_gate,
    w_up,
    w_down,
):
    devices = lax.axis_size("shard")
    me = lax.axis_index("shard")
    tok_dev, depth = hidden.shape
    topk = route_ids.shape[1]
    local = w_gate.shape[0]
    experts = local * devices
    capacity = max(2, tok_dev * topk * 5 // (4 * experts))
    capacity = -(-capacity // 16) * 16

    ids_all = lax.all_gather(route_ids, "shard", axis=0)
    weights_all = lax.all_gather(route_weights, "shard", axis=0)
    live_all = jnp.arange(devices * tok_dev, dtype=jnp.int32).reshape(devices, tok_dev) < counts[0]
    info = []
    for e in range(local):
        info.append(jnp.sum((ids_all == me * local + e).astype(jnp.float32), axis=2))
    for e in range(local):
        matched = jnp.where(ids_all == me * local + e, weights_all.astype(jnp.float32), 0.0)
        info.append(jnp.where(live_all, jnp.sum(matched, axis=2), 0.0))
    info = jnp.stack(info, axis=1)
    info = jnp.pad(info, ((0, 0), (0, -info.shape[1] % 8), (0, 0)))

    both = ring_gather(jnp.concatenate([key_rows, value_rows], axis=1), devices, 0)
    both = both.reshape(devices * tok_dev, both.shape[2])
    first = (me * tok_dev).astype(jnp.int32).reshape(1)
    attended = attend(counts, first, query_rows, both)
    out_all = ring_gather(out_weight, devices, 1).reshape(-1, depth)
    mixed_rows = hidden.astype(jnp.float32) + jnp.dot(
        attended, out_all, preferred_element_type=jnp.float32
    )
    mean_square = jnp.mean(mixed_rows * mixed_rows, axis=1, keepdims=True)
    normed = (mixed_rows * lax.rsqrt(mean_square + 1e-06) * norm_gain.astype(jnp.float32)).astype(
        jnp.bfloat16
    )
    normed_all = ring_gather(normed, devices, 2)
    sums = expert_sums(counts, normed_all, info, w_gate, w_up, w_down, capacity)
    summed = lax.psum_scatter(
        sums.reshape(devices * tok_dev, depth), "shard", scatter_dimension=0, tiled=True
    )
    return (mixed_rows + summed.astype(jnp.float32)).astype(jnp.bfloat16)


def solution(mesh):
    rows = P(("groups", "shard"), None)
    weights = P("shard", None, None)
    return jax.shard_map(
        per_device,
        mesh=mesh,
        in_specs=(
            rows,
            rows,
            rows,
            rows,
            P("groups"),
            P("shard", None),
            P(),
            rows,
            rows,
            weights,
            weights,
            weights,
        ),
        out_specs=rows,
        check_vma=False,
    )
```

```python
import functools
import math

import jax
import jax.numpy as jnp
from jax import lax
from jax.experimental import pallas as pl
from jax.experimental.pallas import tpu as pltpu
from jax.sharding import PartitionSpec as P

HD = 128
SEQ_LEN = 4096
NEG = -1e30
MESH = pl.DeviceIdType.MESH


def ring_place(chips, index):
    if chips == 8:
        z, y = index // 2, index % 2
        return z + y * (7 - 2 * z)
    return index


def ring_chip(chips, place):
    if chips == 8:
        half = place // 4
        z = place + half * (7 - 2 * place)
        return 2 * z + half
    return place


def gather_kernel(devices, pieces, x_ref, o_ref, local_sem, near_send, near_recv, send, recv):
    chips = devices // 2
    me = lax.axis_index("shard")
    group = lax.axis_index("groups")
    core = me % 2
    place = ring_place(chips, me // 2)

    def device_at(offset):
        return ring_chip(chips, (place + offset + 2 * chips) % chips) * 2 + core

    right, left, sibling = device_at(1), device_at(-1), me + 1 - 2 * core
    barrier = pltpu.get_barrier_semaphore()
    for other in (right, left, sibling):
        pl.semaphore_signal(barrier, inc=1, device_id=(group, other), device_id_type=MESH)
    pl.semaphore_wait(barrier, 3)

    rows = x_ref.shape[0] // (2 * pieces)

    def part(ref, way, piece):
        return ref.at[pl.ds((way * pieces + piece) * rows, rows)]

    def hop(step, way, piece):
        origin = device_at(-step if way == 0 else step)
        src = part(x_ref if step == 0 else o_ref.at[origin], way, piece)
        return pltpu.make_async_remote_copy(
            src_ref=src,
            dst_ref=part(o_ref.at[origin], way, piece),
            send_sem=send.at[step, way, piece],
            recv_sem=recv.at[step, way, piece],
            device_id=(group, right if way == 0 else left),
            device_id_type=MESH,
        )

    def landing(step, way, piece):
        origin = device_at(-step - 1 if way == 0 else step + 1)
        place_of = part(o_ref.at[origin], way, piece)
        return pltpu.make_async_remote_copy(
            src_ref=place_of,
            dst_ref=place_of,
            send_sem=send.at[step, way, piece],
            recv_sem=recv.at[step, way, piece],
            device_id=(group, right if way == 0 else left),
            device_id_type=MESH,
        )

    def near(step, way, piece):
        if step < 0:
            src, origin = part(x_ref, way, piece), me
        else:
            origin = device_at(-step - 1 if way == 0 else step + 1)
            src = part(o_ref.at[origin], way, piece)
        return pltpu.make_async_remote_copy(
            src_ref=src,
            dst_ref=part(o_ref.at[origin], way, piece),
            send_sem=near_send.at[step + 1, way, piece],
            recv_sem=near_recv.at[step + 1, way, piece],
            device_id=(group, sibling),
            device_id_type=MESH,
        )

    def near_landing(step, way, piece):
        if step < 0:
            origin = sibling
        else:
            origin = device_at(-step - 1 if way == 0 else step + 1) + 1 - 2 * core
        place_of = part(o_ref.at[origin], way, piece)
        return pltpu.make_async_remote_copy(
            src_ref=place_of,
            dst_ref=place_of,
            send_sem=near_send.at[step + 1, way, piece],
            recv_sem=near_recv.at[step + 1, way, piece],
            device_id=(group, sibling),
            device_id_type=MESH,
        )

    every = [(way, piece) for piece in range(pieces) for way in range(2)]
    for way, piece in every:
        hop(0, way, piece).start()
    own = pltpu.make_async_copy(x_ref, o_ref.at[me], local_sem)
    own.start()
    for way, piece in every:
        near(-1, way, piece).start()
    for step in range(chips - 1):
        for way, piece in every:
            landing(step, way, piece).wait_recv()
            if step + 1 < chips - 1:
                hop(step + 1, way, piece).start()
            near(step, way, piece).start()
    own.wait()
    for step in range(chips - 1):
        for way, piece in every:
            hop(step, way, piece).wait_send()
    for step in range(-1, chips - 1):
        for way, piece in every:
            near(step, way, piece).wait_send()
            near_landing(step, way, piece).wait_recv()


def ring_gather(x, devices, collective_id, pieces=2):
    steps = devices // 2
    dma = pltpu.SemaphoreType.DMA
    return pl.pallas_call(
        functools.partial(gather_kernel, devices, pieces),
        out_shape=jax.ShapeDtypeStruct((devices,) + x.shape, x.dtype),
        in_specs=[pl.BlockSpec(memory_space=pltpu.HBM)],
        out_specs=pl.BlockSpec(memory_space=pltpu.HBM),
        scratch_shapes=[
            dma,
            dma((steps, 2, pieces)),
            dma((steps, 2, pieces)),
            dma((steps, 2, pieces)),
            dma((steps, 2, pieces)),
        ],
        compiler_params=pltpu.CompilerParams(collective_id=collective_id, has_side_effects=True),
    )(x)


def scatter_kernel(
    devices, pieces, x_ref, o_ref, held, near_in, ring_in, load, near_send, near_recv, send, recv
):
    chips = devices // 2
    me = lax.axis_index("shard")
    group = lax.axis_index("groups")
    core = me % 2
    place = ring_place(chips, me // 2)

    def chip_at(offset):
        return ring_chip(chips, (place + offset + 2 * chips) % chips) * 2

    right, left, sibling = chip_at(1) + core, chip_at(-1) + core, me + 1 - 2 * core
    barrier = pltpu.get_barrier_semaphore()
    for other in (right, left, sibling):
        pl.semaphore_signal(barrier, inc=1, device_id=(group, other), device_id_type=MESH)
    pl.semaphore_wait(barrier, 3)

    rows = x_ref.shape[1] // (2 * pieces)
    every = [(way, piece) for piece in range(pieces) for way in range(2)]

    def span(way, piece):
        return pl.ds((way * pieces + piece) * rows, rows)

    def target(step, way):
        return chip_at(-step - 1 if way == 0 else step + 1)

    def fetch(step, way, piece):
        return pltpu.make_async_copy(
            x_ref.at[target(step, way) + core, span(way, piece)],
            held.at[step, span(way, piece)],
            load.at[step, way, piece],
        )

    def near(step, way, piece):
        return pltpu.make_async_remote_copy(
            src_ref=x_ref.at[target(step, way) + 1 - core, span(way, piece)],
            dst_ref=near_in.at[step, span(way, piece)],
            send_sem=near_send.at[step, way, piece],
            recv_sem=near_recv.at[step, way, piece],
            device_id=(group, sibling),
            device_id_type=MESH,
        )

    def hop(step, way, piece):
        return pltpu.make_async_remote_copy(
            src_ref=held.at[step, span(way, piece)],
            dst_ref=ring_in.at[step, span(way, piece)],
            send_sem=send.at[step, way, piece],
            recv_sem=recv.at[step, way, piece],
            device_id=(group, right if way == 0 else left),
            device_id_type=MESH,
        )

    for step in range(chips):
        for way, piece in every:
            near(step, way, piece).start()
            fetch(step, way, piece).start()
    for step in range(chips):
        for way, piece in every:
            here = span(way, piece)
            fetch(step, way, piece).wait()
            near(step, way, piece).wait_recv()
            total = held[step, here, :].astype(jnp.float32) + near_in[step, here, :].astype(
                jnp.float32
            )
            if step > 0:
                hop(step - 1, way, piece).wait_recv()
                total = total + ring_in[step - 1, here, :].astype(jnp.float32)
            if step < chips - 1:
                held[step, here, :] = total.astype(held.dtype)
                hop(step, way, piece).start()
            else:
                o_ref[here, :] = total.astype(o_ref.dtype)
    for step in range(chips):
        for way, piece in every:
            near(step, way, piece).wait_send()
            if step < chips - 1:
                hop(step, way, piece).wait_send()


def ring_scatter(x, collective_id, pieces=2):
    devices, rows, depth = x.shape
    chips = devices // 2
    dma = pltpu.SemaphoreType.DMA
    sems = dma((chips, 2, pieces))
    return pl.pallas_call(
        functools.partial(scatter_kernel, devices, pieces),
        out_shape=jax.ShapeDtypeStruct((rows, depth), x.dtype),
        in_specs=[pl.BlockSpec(memory_space=pltpu.HBM)],
        out_specs=pl.BlockSpec(memory_space=pltpu.VMEM),
        scratch_shapes=[pltpu.VMEM((chips, rows, depth), x.dtype)] * 2
        + [pltpu.VMEM((chips - 1, rows, depth), x.dtype)]
        + [sems] * 5,
        compiler_params=pltpu.CompilerParams(
            collective_id=collective_id, has_side_effects=True, vmem_limit_bytes=40 << 20
        ),
    )(x)


def attend_kernel(step_rows, heads, count_ref, first_ref, q_ref, k_ref, v_ref, o_ref, qs, top, total):
    rows = q_ref.shape[0]
    scale = math.log2(math.e) / math.sqrt(HD)
    count = count_ref[0]
    first = first_ref[0]
    seen = jnp.minimum(count, first + rows)
    blocks = jnp.where(first < count, (seen + step_rows - 1) // step_rows, 0)
    for h in range(heads):
        qs[h * rows : (h + 1) * rows, :] = q_ref[:, h * HD : (h + 1) * HD]
    top[...] = jnp.full(top.shape, NEG, jnp.float32)
    total[...] = jnp.zeros(total.shape, jnp.float32)
    ones = jnp.ones((step_rows, HD), jnp.bfloat16)

    def fold(start, masked):
        start = pl.multiple_of(start, step_rows)
        keys = k_ref[pl.ds(start, step_rows), :]
        values = jnp.concatenate([v_ref[pl.ds(start, step_rows), :], ones], axis=1)
        if masked:
            at_row = first + lax.broadcasted_iota(jnp.int32, (rows, step_rows), 0)
            at_col = start + lax.broadcasted_iota(jnp.int32, (rows, step_rows), 1)
            visible = (at_col <= at_row) & (at_col < count)
        for h in range(heads):
            span = slice(h * rows, (h + 1) * rows)
            scores = lax.dot_general(
                qs[span, :], keys, (((1,), (1,)), ((), ())), preferred_element_type=jnp.float32
            )
            if masked:
                scores = jnp.where(visible, scores, NEG)
            old = top[span, :]
            new = jnp.maximum(old, jnp.max(scores, axis=1, keepdims=True) * scale)
            expo = jnp.exp2(scores * scale - new[:, :1]).astype(jnp.bfloat16)
            factor = jnp.exp2(old - new)
            part = jnp.dot(expo, values, preferred_element_type=jnp.float32)
            total[span, :] = total[span, :] * jnp.concatenate([factor, factor], axis=1) + part
            top[span, :] = new

    def body(i, carry):
        fold(i * step_rows, False)
        return carry

    lax.fori_loop(0, blocks - 1, body, 0)

    @pl.when(blocks > 0)
    def _():
        fold((blocks - 1) * step_rows, True)

    live = first + lax.broadcasted_iota(jnp.int32, (rows, HD), 0) < count
    for h in range(heads):
        both = total[h * rows : (h + 1) * rows, :]
        result = jnp.where(live, both[:, :HD] / jnp.where(live, both[:, HD:], 1.0), 0.0)
        o_ref[:, h * HD : (h + 1) * HD] = result.astype(jnp.bfloat16)


def attend(count, first, queries, keys_values, kv_count):
    rows, width = queries.shape
    length = keys_values.shape[0]
    heads = width // HD // kv_count
    step_rows = math.gcd(length, 512)
    smem = pl.BlockSpec(memory_space=pltpu.SMEM)
    return pl.pallas_call(
        functools.partial(attend_kernel, step_rows, heads),
        grid=(kv_count,),
        out_shape=jax.ShapeDtypeStruct((rows, width), jnp.bfloat16),
        in_specs=[
            smem,
            smem,
            pl.BlockSpec((rows, heads * HD), lambda g: (0, g)),
            pl.BlockSpec((length, HD), lambda g: (0, g)),
            pl.BlockSpec((length, HD), lambda g: (0, kv_count + g)),
        ],
        out_specs=pl.BlockSpec((rows, heads * HD), lambda g: (0, g)),
        scratch_shapes=[
            pltpu.VMEM((heads * rows, HD), jnp.bfloat16),
            pltpu.VMEM((heads * rows, HD), jnp.float32),
            pltpu.VMEM((heads * rows, 2 * HD), jnp.float32),
        ],
        compiler_params=pltpu.CompilerParams(vmem_limit_bytes=40 << 20),
        cost_estimate=pl.CostEstimate(
            flops=4 * rows * width * length, bytes_accessed=12 << 20, transcendentals=rows * width * length // HD
        ),
    )(count, first, queries, keys_values, keys_values)


def expert_kernel(local, cap, per, count_ref, x_ref, info_ref, wg_ref, wu_ref, wd_ref, o_ref, picked, given):
    rows = x_ref.shape[1]
    start = pl.program_id(0) * per * rows
    alive = start % SEQ_LEN < count_ref[0]

    @pl.when(jnp.logical_not(alive))
    def _():
        o_ref[...] = jnp.zeros(o_ref.shape, o_ref.dtype)

    @pl.when(alive)
    def _():
        before = (
            lax.broadcasted_iota(jnp.int32, (rows, rows), 0)
            < lax.broadcasted_iota(jnp.int32, (rows, rows), 1)
        ).astype(jnp.bfloat16)
        slot_at = lax.broadcasted_iota(jnp.int32, (cap, rows), 0).astype(jnp.float32)
        choices = []
        weights = [[] for _ in range(local)]
        for b in range(per):
            info = info_ref[b]
            slots = jnp.dot(info.astype(jnp.bfloat16), before, preferred_element_type=jnp.float32)
            mine = []
            for e in range(local):
                hit = (slot_at == slots[e : e + 1]) & (info[e : e + 1] > 0.5)
                mine.append(jnp.where(hit, 1.0, 0.0))
                weights[e].append(
                    jnp.sum(
                        jnp.where(hit, info[local + e : local + e + 1], 0.0), axis=1, keepdims=True
                    )
                )
            choice = jnp.concatenate(mine, axis=0).astype(jnp.bfloat16)
            choices.append(choice)
            rows_here = jnp.dot(choice, x_ref[b], preferred_element_type=jnp.float32)
            rows_here = rows_here.astype(jnp.bfloat16)
            for e in range(local):
                picked[e, b * cap : (b + 1) * cap, :] = rows_here[e * cap : (e + 1) * cap]
        for e in range(local):
            mine = picked[e]
            gate = jnp.dot(mine, wg_ref[e], preferred_element_type=jnp.float32)
            up = jnp.dot(mine, wu_ref[e], preferred_element_type=jnp.float32)
            act = (gate / (1.0 + jnp.exp(-gate)) * up).astype(jnp.bfloat16)
            down = jnp.dot(act, wd_ref[e], preferred_element_type=jnp.float32)
            down = (down * jnp.concatenate(weights[e], axis=0)).astype(jnp.bfloat16)
            for b in range(per):
                given[b, e * cap : (e + 1) * cap, :] = down[b * cap : (b + 1) * cap]
        for b in range(per):
            back = lax.dot_general(
                choices[b], given[b], (((0,), (0,)), ((), ())), preferred_element_type=jnp.float32
            )
            o_ref[b] = back.astype(o_ref.dtype)


def expert_sums(count, rows_all, info, w_gate, w_up, w_down, cap):
    devices, rows, depth = rows_all.shape
    local, _, hidden_units = w_gate.shape
    per = 4
    whole = pl.Buffered(1)
    return pl.pallas_call(
        functools.partial(expert_kernel, local, cap, per),
        grid=(devices // per,),
        out_shape=jax.ShapeDtypeStruct((devices, rows, depth), jnp.bfloat16),
        in_specs=[
            pl.BlockSpec(memory_space=pltpu.SMEM),
            pl.BlockSpec((per, rows, depth), lambda i: (i, 0, 0)),
            pl.BlockSpec((per,) + info.shape[1:], lambda i: (i, 0, 0)),
            pl.BlockSpec(w_gate.shape, lambda i: (0, 0, 0), pipeline_mode=whole),
            pl.BlockSpec(w_up.shape, lambda i: (0, 0, 0), pipeline_mode=whole),
            pl.BlockSpec(w_down.shape, lambda i: (0, 0, 0), pipeline_mode=whole),
        ],
        out_specs=pl.BlockSpec((per, rows, depth), lambda i: (i, 0, 0)),
        scratch_shapes=[
            pltpu.VMEM((local, per * cap, depth), jnp.bfloat16),
            pltpu.VMEM((per, local * cap, depth), jnp.bfloat16),
        ],
        compiler_params=pltpu.CompilerParams(vmem_limit_bytes=60 << 20),
    )(count, rows_all, info, w_gate, w_up, w_down)


def per_device(
    hidden,
    query_rows,
    key_rows,
    value_rows,
    counts,
    out_weight,
    norm_gain,
    route_ids,
    route_weights,
    w_gate,
    w_up,
    w_down,
):
    devices = lax.axis_size("shard")
    me = lax.axis_index("shard")
    tok_dev, depth = hidden.shape
    topk = route_ids.shape[1]
    local = w_gate.shape[0]
    experts = local * devices
    capacity = max(2, tok_dev * topk * 5 // (4 * experts))
    capacity = -(-capacity // 16) * 16

    kv_width = 2 * key_rows.shape[1]
    routing = jnp.concatenate([route_ids.astype(jnp.bfloat16), route_weights], axis=1)
    routing = jnp.pad(routing, ((0, 0), (0, HD - 2 * topk)))
    both = ring_gather(jnp.concatenate([key_rows, value_rows, routing], axis=1), devices, 0)
    ids_all = both[:, :, kv_width : kv_width + topk].astype(jnp.int32)
    weights_all = both[:, :, kv_width + topk : kv_width + 2 * topk]
    live_all = jnp.arange(devices * tok_dev, dtype=jnp.int32).reshape(devices, tok_dev) < counts[0]
    info = []
    for e in range(local):
        info.append(jnp.sum((ids_all == me * local + e).astype(jnp.float32), axis=2))
    for e in range(local):
        matched = jnp.where(ids_all == me * local + e, weights_all.astype(jnp.float32), 0.0)
        info.append(jnp.where(live_all, jnp.sum(matched, axis=2), 0.0))
    info = jnp.stack(info, axis=1)
    info = jnp.pad(info, ((0, 0), (0, -info.shape[1] % 8), (0, 0)))

    both = both.reshape(devices * tok_dev, both.shape[2])
    first = (me * tok_dev).astype(jnp.int32).reshape(1)
    attended = attend(counts, first, query_rows, both, key_rows.shape[1] // HD)
    out_all = ring_gather(out_weight, devices, 1).reshape(-1, depth)
    mixed_rows = hidden.astype(jnp.float32) + jnp.dot(
        attended, out_all, preferred_element_type=jnp.float32
    )
    mean_square = jnp.mean(mixed_rows * mixed_rows, axis=1, keepdims=True)
    normed = (mixed_rows * lax.rsqrt(mean_square + 1e-06) * norm_gain.astype(jnp.float32)).astype(
        jnp.bfloat16
    )
    normed_all = ring_gather(normed, devices, 2)
    sums = expert_sums(counts, normed_all, info, w_gate, w_up, w_down, capacity)
    summed = ring_scatter(sums, 3)
    return (mixed_rows + summed.astype(jnp.float32)).astype(jnp.bfloat16)


def solution(mesh):
    rows = P(("groups", "shard"), None)
    weights = P("shard", None, None)
    return jax.shard_map(
        per_device,
        mesh=mesh,
        in_specs=(
            rows,
            rows,
            rows,
            rows,
            P("groups"),
            P("shard", None),
            P(),
            rows,
            rows,
            weights,
            weights,
            weights,
        ),
        out_specs=rows,
        check_vma=False,
    )
```

```python
import functools
import math

import jax
import jax.numpy as jnp
from jax import lax
from jax.experimental import pallas as pl
from jax.experimental.pallas import tpu as pltpu
from jax.sharding import PartitionSpec as P

HD = 128
SEQ_LEN = 4096
NEG = -1e30
MESH = pl.DeviceIdType.MESH


def ring_place(chips, index):
    if chips == 8:
        z, y = index // 2, index % 2
        return z + y * (7 - 2 * z)
    return index


def ring_chip(chips, place):
    if chips == 8:
        half = place // 4
        z = place + half * (7 - 2 * place)
        return 2 * z + half
    return place


def gather_moves(devices, pieces, x_ref, o_ref, local_sem, near_send, near_recv, send, recv):
    chips = devices // 2
    me = lax.axis_index("shard")
    group = lax.axis_index("groups")
    core = me % 2
    place = ring_place(chips, me // 2)

    def device_at(offset):
        return ring_chip(chips, (place + offset + 2 * chips) % chips) * 2 + core

    right, left, sibling = device_at(1), device_at(-1), me + 1 - 2 * core
    rows = x_ref.shape[0] // (2 * pieces)

    def part(ref, way, piece):
        return ref.at[pl.ds((way * pieces + piece) * rows, rows)]

    def hop(step, way, piece):
        origin = device_at(-step if way == 0 else step)
        src = part(x_ref if step == 0 else o_ref.at[origin], way, piece)
        return pltpu.make_async_remote_copy(
            src_ref=src,
            dst_ref=part(o_ref.at[origin], way, piece),
            send_sem=send.at[step, way, piece],
            recv_sem=recv.at[step, way, piece],
            device_id=(group, right if way == 0 else left),
            device_id_type=MESH,
        )

    def landing(step, way, piece):
        origin = device_at(-step - 1 if way == 0 else step + 1)
        place_of = part(o_ref.at[origin], way, piece)
        return pltpu.make_async_remote_copy(
            src_ref=place_of,
            dst_ref=place_of,
            send_sem=send.at[step, way, piece],
            recv_sem=recv.at[step, way, piece],
            device_id=(group, right if way == 0 else left),
            device_id_type=MESH,
        )

    def near(step, way, piece):
        if step < 0:
            src, origin = part(x_ref, way, piece), me
        else:
            origin = device_at(-step - 1 if way == 0 else step + 1)
            src = part(o_ref.at[origin], way, piece)
        return pltpu.make_async_remote_copy(
            src_ref=src,
            dst_ref=part(o_ref.at[origin], way, piece),
            send_sem=near_send.at[step + 1, way, piece],
            recv_sem=near_recv.at[step + 1, way, piece],
            device_id=(group, sibling),
            device_id_type=MESH,
        )

    def near_landing(step, way, piece):
        if step < 0:
            origin = sibling
        else:
            origin = device_at(-step - 1 if way == 0 else step + 1) + 1 - 2 * core
        place_of = part(o_ref.at[origin], way, piece)
        return pltpu.make_async_remote_copy(
            src_ref=place_of,
            dst_ref=place_of,
            send_sem=near_send.at[step + 1, way, piece],
            recv_sem=near_recv.at[step + 1, way, piece],
            device_id=(group, sibling),
            device_id_type=MESH,
        )

    every = [(way, piece) for piece in range(pieces) for way in range(2)]
    own = pltpu.make_async_copy(x_ref, o_ref.at[me], local_sem)

    def begin():
        barrier = pltpu.get_barrier_semaphore()
        for other in (right, left, sibling):
            pl.semaphore_signal(barrier, inc=1, device_id=(group, other), device_id_type=MESH)
        pl.semaphore_wait(barrier, 3)
        for way, piece in every:
            hop(0, way, piece).start()
        own.start()
        for way, piece in every:
            near(-1, way, piece).start()

    def stage(step):
        for way, piece in every:
            landing(step, way, piece).wait_recv()
            if step + 1 < chips - 1:
                hop(step + 1, way, piece).start()
            near(step, way, piece).start()

    def finish():
        own.wait()
        for step in range(chips - 1):
            for way, piece in every:
                hop(step, way, piece).wait_send()
        for step in range(-1, chips - 1):
            for way, piece in every:
                near(step, way, piece).wait_send()
                near_landing(step, way, piece).wait_recv()

    return begin, stage, finish


def gather_kernel(devices, pieces, x_ref, o_ref, *sems):
    begin, stage, finish = gather_moves(devices, pieces, x_ref, o_ref, *sems)
    begin()
    for step in range(devices // 2 - 1):
        stage(step)
    finish()


def gather_scratch(devices, pieces):
    dma = pltpu.SemaphoreType.DMA
    return [dma] + [dma((devices // 2, 2, pieces))] * 4


def ring_gather(x, devices, collective_id, pieces=2):
    return pl.pallas_call(
        functools.partial(gather_kernel, devices, pieces),
        out_shape=jax.ShapeDtypeStruct((devices,) + x.shape, x.dtype),
        in_specs=[pl.BlockSpec(memory_space=pltpu.HBM)],
        out_specs=pl.BlockSpec(memory_space=pltpu.HBM),
        scratch_shapes=gather_scratch(devices, pieces),
        compiler_params=pltpu.CompilerParams(collective_id=collective_id, has_side_effects=True),
    )(x)


def scatter_kernel(
    devices, pieces, x_ref, o_ref, held, near_in, ring_in, load, near_send, near_recv, send, recv
):
    chips = devices // 2
    me = lax.axis_index("shard")
    group = lax.axis_index("groups")
    core = me % 2
    place = ring_place(chips, me // 2)

    def chip_at(offset):
        return ring_chip(chips, (place + offset + 2 * chips) % chips) * 2

    right, left, sibling = chip_at(1) + core, chip_at(-1) + core, me + 1 - 2 * core
    barrier = pltpu.get_barrier_semaphore()
    for other in (right, left, sibling):
        pl.semaphore_signal(barrier, inc=1, device_id=(group, other), device_id_type=MESH)
    pl.semaphore_wait(barrier, 3)

    rows = x_ref.shape[1] // (2 * pieces)
    every = [(way, piece) for piece in range(pieces) for way in range(2)]

    def span(way, piece):
        return pl.ds((way * pieces + piece) * rows, rows)

    def target(step, way):
        return chip_at(-step - 1 if way == 0 else step + 1)

    def fetch(step, way, piece):
        return pltpu.make_async_copy(
            x_ref.at[target(step, way) + core, span(way, piece)],
            held.at[step, span(way, piece)],
            load.at[step, way, piece],
        )

    def near(step, way, piece):
        return pltpu.make_async_remote_copy(
            src_ref=x_ref.at[target(step, way) + 1 - core, span(way, piece)],
            dst_ref=near_in.at[step, span(way, piece)],
            send_sem=near_send.at[step, way, piece],
            recv_sem=near_recv.at[step, way, piece],
            device_id=(group, sibling),
            device_id_type=MESH,
        )

    def hop(step, way, piece):
        return pltpu.make_async_remote_copy(
            src_ref=held.at[step, span(way, piece)],
            dst_ref=ring_in.at[step, span(way, piece)],
            send_sem=send.at[step, way, piece],
            recv_sem=recv.at[step, way, piece],
            device_id=(group, right if way == 0 else left),
            device_id_type=MESH,
        )

    for step in range(chips):
        for way, piece in every:
            near(step, way, piece).start()
            fetch(step, way, piece).start()
    for step in range(chips):
        for way, piece in every:
            here = span(way, piece)
            fetch(step, way, piece).wait()
            near(step, way, piece).wait_recv()
            total = held[step, here, :].astype(jnp.float32) + near_in[step, here, :].astype(
                jnp.float32
            )
            if step > 0:
                hop(step - 1, way, piece).wait_recv()
                total = total + ring_in[step - 1, here, :].astype(jnp.float32)
            if step < chips - 1:
                held[step, here, :] = total.astype(held.dtype)
                hop(step, way, piece).start()
            else:
                o_ref[here, :] = total.astype(o_ref.dtype)
    for step in range(chips):
        for way, piece in every:
            near(step, way, piece).wait_send()
            if step < chips - 1:
                hop(step, way, piece).wait_send()


def ring_scatter(x, collective_id, pieces=2):
    devices, rows, depth = x.shape
    chips = devices // 2
    dma = pltpu.SemaphoreType.DMA
    sems = dma((chips, 2, pieces))
    return pl.pallas_call(
        functools.partial(scatter_kernel, devices, pieces),
        out_shape=jax.ShapeDtypeStruct((rows, depth), x.dtype),
        in_specs=[pl.BlockSpec(memory_space=pltpu.HBM)],
        out_specs=pl.BlockSpec(memory_space=pltpu.VMEM),
        scratch_shapes=[pltpu.VMEM((chips, rows, depth), x.dtype)] * 2
        + [pltpu.VMEM((chips - 1, rows, depth), x.dtype)]
        + [sems] * 5,
        compiler_params=pltpu.CompilerParams(
            collective_id=collective_id, has_side_effects=True, vmem_limit_bytes=40 << 20
        ),
    )(x)


def attend_kernel(
    devices, pieces, step_rows, heads, groups,
    count_ref, q_ref, k_ref, v_ref, w_ref, o_ref, all_ref, qs, top, total, *sems
):
    begin, stage, finish = gather_moves(devices, pieces, w_ref, all_ref, *sems)
    rows = q_ref.shape[0]
    scale = math.log2(math.e) / math.sqrt(HD)
    count = count_ref[0]
    first = lax.axis_index("shard") * rows
    blocks = (first + rows + step_rows - 1) // step_rows
    j = pl.program_id(1)
    steps = k_ref.shape[0] // step_rows
    at_step = pl.program_id(0) * steps + j
    all_steps = groups * steps

    @pl.when(at_step == 0)
    def _():
        begin()

    @pl.when(j == 0)
    def _():
        for h in range(heads):
            qs[h * rows : (h + 1) * rows, :] = q_ref[:, h * HD : (h + 1) * HD]
        top[...] = jnp.full(top.shape, NEG, jnp.float32)
        total[...] = jnp.zeros(total.shape, jnp.float32)

    def fold(masked):
        start = pl.multiple_of(j * step_rows, step_rows)
        keys = k_ref[pl.ds(start, step_rows), :]
        ones = jnp.ones((step_rows, HD), jnp.bfloat16)
        values = jnp.concatenate([v_ref[pl.ds(start, step_rows), :], ones], axis=1)
        if masked:
            at_row = first + lax.broadcasted_iota(jnp.int32, (rows, step_rows), 0)
            at_col = start + lax.broadcasted_iota(jnp.int32, (rows, step_rows), 1)
            visible = (at_col <= at_row) & (at_col < count)
        for h in range(heads):
            span = slice(h * rows, (h + 1) * rows)
            scores = lax.dot_general(
                qs[span, :], keys, (((1,), (1,)), ((), ())), preferred_element_type=jnp.float32
            )
            if masked:
                scores = jnp.where(visible, scores, NEG)
            old = top[span, :]
            new = jnp.maximum(old, jnp.max(scores, axis=1, keepdims=True) * scale)
            expo = jnp.exp2(scores * scale - new[:, :1]).astype(jnp.bfloat16)
            factor = jnp.exp2(old - new)
            part = jnp.dot(expo, values, preferred_element_type=jnp.float32)
            total[span, :] = total[span, :] * jnp.concatenate([factor, factor], axis=1) + part
            top[span, :] = new

    @pl.when(j < blocks - 1)
    def _():
        fold(False)

    @pl.when(j == blocks - 1)
    def _():
        fold(True)

        live = first + lax.broadcasted_iota(jnp.int32, (rows, HD), 0) < count
        for h in range(heads):
            both = total[h * rows : (h + 1) * rows, :]
            result = jnp.where(live, both[:, :HD] / jnp.where(live, both[:, HD:], 1.0), 0.0)
            o_ref[:, h * HD : (h + 1) * HD] = result.astype(jnp.bfloat16)

    stages = devices // 2 - 1
    for number in range(stages):

        @pl.when(at_step == (number + 1) * all_steps // stages - 1)
        def _(number=number):
            stage(number)

    @pl.when(at_step == all_steps - 1)
    def _():
        finish()


def attend(count, queries, keys_values, out_weight, kv_count, devices, collective_id, pieces=2):
    rows, width = queries.shape
    length = keys_values.shape[0]
    heads = width // HD // kv_count
    step_rows = math.gcd(length, 512)
    hbm = pl.BlockSpec(memory_space=pltpu.HBM)
    return pl.pallas_call(
        functools.partial(attend_kernel, devices, pieces, step_rows, heads, kv_count),
        grid=(kv_count, length // step_rows),
        out_shape=(
            jax.ShapeDtypeStruct((rows, width), jnp.bfloat16),
            jax.ShapeDtypeStruct((devices,) + out_weight.shape, jnp.bfloat16),
        ),
        in_specs=[
            pl.BlockSpec(memory_space=pltpu.SMEM),
            pl.BlockSpec((rows, heads * HD), lambda g, j: (0, g)),
            pl.BlockSpec((length, HD), lambda g, j: (0, g)),
            pl.BlockSpec((length, HD), lambda g, j: (0, kv_count + g)),
            hbm,
        ],
        out_specs=(pl.BlockSpec((rows, heads * HD), lambda g, j: (0, g)), hbm),
        scratch_shapes=[
            pltpu.VMEM((heads * rows, HD), jnp.bfloat16),
            pltpu.VMEM((heads * rows, HD), jnp.float32),
            pltpu.VMEM((heads * rows, 2 * HD), jnp.float32),
        ]
        + gather_scratch(devices, pieces),
        compiler_params=pltpu.CompilerParams(
            collective_id=collective_id, has_side_effects=True, vmem_limit_bytes=40 << 20
        ),
    )(count, queries, keys_values, keys_values, out_weight)


def expert_kernel(local, cap, per, count_ref, x_ref, info_ref, wg_ref, wu_ref, wd_ref, o_ref, picked, given):
    rows = x_ref.shape[1]
    start = pl.program_id(0) * per * rows
    alive = start % SEQ_LEN < count_ref[0]

    @pl.when(jnp.logical_not(alive))
    def _():
        o_ref[...] = jnp.zeros(o_ref.shape, o_ref.dtype)

    @pl.when(alive)
    def _():
        before = (
            lax.broadcasted_iota(jnp.int32, (rows, rows), 0)
            < lax.broadcasted_iota(jnp.int32, (rows, rows), 1)
        ).astype(jnp.bfloat16)
        slot_at = lax.broadcasted_iota(jnp.int32, (cap, rows), 0).astype(jnp.float32)
        choices = []
        weights = [[] for _ in range(local)]
        for b in range(per):
            info = info_ref[b]
            slots = jnp.dot(info.astype(jnp.bfloat16), before, preferred_element_type=jnp.float32)
            mine = []
            for e in range(local):
                hit = (slot_at == slots[e : e + 1]) & (info[e : e + 1] > 0.5)
                mine.append(jnp.where(hit, 1.0, 0.0))
                weights[e].append(
                    jnp.sum(
                        jnp.where(hit, info[local + e : local + e + 1], 0.0), axis=1, keepdims=True
                    )
                )
            choice = jnp.concatenate(mine, axis=0).astype(jnp.bfloat16)
            choices.append(choice)
            rows_here = jnp.dot(choice, x_ref[b], preferred_element_type=jnp.float32)
            rows_here = rows_here.astype(jnp.bfloat16)
            for e in range(local):
                picked[e, b * cap : (b + 1) * cap, :] = rows_here[e * cap : (e + 1) * cap]
        for e in range(local):
            mine = picked[e]
            gate = jnp.dot(mine, wg_ref[e], preferred_element_type=jnp.float32)
            up = jnp.dot(mine, wu_ref[e], preferred_element_type=jnp.float32)
            act = (gate / (1.0 + jnp.exp(-gate)) * up).astype(jnp.bfloat16)
            down = jnp.dot(act, wd_ref[e], preferred_element_type=jnp.float32)
            down = (down * jnp.concatenate(weights[e], axis=0)).astype(jnp.bfloat16)
            for b in range(per):
                given[b, e * cap : (e + 1) * cap, :] = down[b * cap : (b + 1) * cap]
        for b in range(per):
            back = lax.dot_general(
                choices[b], given[b], (((0,), (0,)), ((), ())), preferred_element_type=jnp.float32
            )
            o_ref[b] = back.astype(o_ref.dtype)


def expert_sums(count, rows_all, info, w_gate, w_up, w_down, cap):
    devices, rows, depth = rows_all.shape
    local, _, hidden_units = w_gate.shape
    per = 4
    whole = pl.Buffered(1)
    return pl.pallas_call(
        functools.partial(expert_kernel, local, cap, per),
        grid=(devices // per,),
        out_shape=jax.ShapeDtypeStruct((devices, rows, depth), jnp.bfloat16),
        in_specs=[
            pl.BlockSpec(memory_space=pltpu.SMEM),
            pl.BlockSpec((per, rows, depth), lambda i: (i, 0, 0)),
            pl.BlockSpec((per,) + info.shape[1:], lambda i: (i, 0, 0)),
            pl.BlockSpec(w_gate.shape, lambda i: (0, 0, 0), pipeline_mode=whole),
            pl.BlockSpec(w_up.shape, lambda i: (0, 0, 0), pipeline_mode=whole),
            pl.BlockSpec(w_down.shape, lambda i: (0, 0, 0), pipeline_mode=whole),
        ],
        out_specs=pl.BlockSpec((per, rows, depth), lambda i: (i, 0, 0)),
        scratch_shapes=[
            pltpu.VMEM((local, per * cap, depth), jnp.bfloat16),
            pltpu.VMEM((per, local * cap, depth), jnp.bfloat16),
        ],
        compiler_params=pltpu.CompilerParams(vmem_limit_bytes=60 << 20),
    )(count, rows_all, info, w_gate, w_up, w_down)


def per_device(
    hidden,
    query_rows,
    key_rows,
    value_rows,
    counts,
    out_weight,
    norm_gain,
    route_ids,
    route_weights,
    w_gate,
    w_up,
    w_down,
):
    devices = lax.axis_size("shard")
    me = lax.axis_index("shard")
    tok_dev, depth = hidden.shape
    topk = route_ids.shape[1]
    local = w_gate.shape[0]
    experts = local * devices
    capacity = max(2, tok_dev * topk * 5 // (4 * experts))
    capacity = -(-capacity // 16) * 16

    kv_width = 2 * key_rows.shape[1]
    routing = jnp.concatenate([route_ids.astype(jnp.bfloat16), route_weights], axis=1)
    routing = jnp.pad(routing, ((0, 0), (0, HD - 2 * topk)))
    both = ring_gather(jnp.concatenate([key_rows, value_rows, routing], axis=1), devices, 0)
    ids_all = both[:, :, kv_width : kv_width + topk].astype(jnp.int32)
    weights_all = both[:, :, kv_width + topk : kv_width + 2 * topk]
    live_all = jnp.arange(devices * tok_dev, dtype=jnp.int32).reshape(devices, tok_dev) < counts[0]
    info = []
    for e in range(local):
        info.append(jnp.sum((ids_all == me * local + e).astype(jnp.float32), axis=2))
    for e in range(local):
        matched = jnp.where(ids_all == me * local + e, weights_all.astype(jnp.float32), 0.0)
        info.append(jnp.where(live_all, jnp.sum(matched, axis=2), 0.0))
    info = jnp.stack(info, axis=1)
    info = jnp.pad(info, ((0, 0), (0, -info.shape[1] % 8), (0, 0)))

    both = both.reshape(devices * tok_dev, both.shape[2])
    attended, out_all = attend(
        counts, query_rows, both, out_weight, key_rows.shape[1] // HD, devices, 1
    )
    out_all = out_all.reshape(-1, depth)
    mixed_rows = hidden.astype(jnp.float32) + jnp.dot(
        attended, out_all, preferred_element_type=jnp.float32
    )
    mean_square = jnp.mean(mixed_rows * mixed_rows, axis=1, keepdims=True)
    normed = (mixed_rows * lax.rsqrt(mean_square + 1e-06) * norm_gain.astype(jnp.float32)).astype(
        jnp.bfloat16
    )
    normed_all = ring_gather(normed, devices, 2)
    sums = expert_sums(counts, normed_all, info, w_gate, w_up, w_down, capacity)
    summed = ring_scatter(sums, 3)
    return (mixed_rows + summed.astype(jnp.float32)).astype(jnp.bfloat16)


def solution(mesh):
    rows = P(("groups", "shard"), None)
    weights = P("shard", None, None)
    return jax.shard_map(
        per_device,
        mesh=mesh,
        in_specs=(
            rows,
            rows,
            rows,
            rows,
            P("groups"),
            P("shard", None),
            P(),
            rows,
            rows,
            weights,
            weights,
            weights,
        ),
        out_specs=rows,
        check_vma=False,
    )
```

```python
import functools
import math

import jax
import jax.numpy as jnp
from jax import lax
from jax.experimental import pallas as pl
from jax.experimental.pallas import tpu as pltpu
from jax.sharding import PartitionSpec as P

HD = 128
SEQ_LEN = 4096
NEG = -1e30
MESH = pl.DeviceIdType.MESH


def ring_place(chips, index):
    if chips == 8:
        z, y = index // 2, index % 2
        return z + y * (7 - 2 * z)
    return index


def ring_chip(chips, place):
    if chips == 8:
        half = place // 4
        z = place + half * (7 - 2 * place)
        return 2 * z + half
    return place


def gather_moves(devices, pieces, x_ref, o_ref, local_sem, near_send, near_recv, send, recv):
    chips = devices // 2
    me = lax.axis_index("shard")
    group = lax.axis_index("groups")
    core = me % 2
    place = ring_place(chips, me // 2)

    def device_at(offset):
        return ring_chip(chips, (place + offset + 2 * chips) % chips) * 2 + core

    right, left, sibling = device_at(1), device_at(-1), me + 1 - 2 * core
    rows = x_ref.shape[0] // (2 * pieces)

    def part(ref, way, piece):
        return ref.at[pl.ds((way * pieces + piece) * rows, rows)]

    def hop(step, way, piece):
        origin = device_at(-step if way == 0 else step)
        src = part(x_ref if step == 0 else o_ref.at[origin], way, piece)
        return pltpu.make_async_remote_copy(
            src_ref=src,
            dst_ref=part(o_ref.at[origin], way, piece),
            send_sem=send.at[step, way, piece],
            recv_sem=recv.at[step, way, piece],
            device_id=(group, right if way == 0 else left),
            device_id_type=MESH,
        )

    def landing(step, way, piece):
        origin = device_at(-step - 1 if way == 0 else step + 1)
        place_of = part(o_ref.at[origin], way, piece)
        return pltpu.make_async_remote_copy(
            src_ref=place_of,
            dst_ref=place_of,
            send_sem=send.at[step, way, piece],
            recv_sem=recv.at[step, way, piece],
            device_id=(group, right if way == 0 else left),
            device_id_type=MESH,
        )

    def near(step, way, piece):
        if step < 0:
            src, origin = part(x_ref, way, piece), me
        else:
            origin = device_at(-step - 1 if way == 0 else step + 1)
            src = part(o_ref.at[origin], way, piece)
        return pltpu.make_async_remote_copy(
            src_ref=src,
            dst_ref=part(o_ref.at[origin], way, piece),
            send_sem=near_send.at[step + 1, way, piece],
            recv_sem=near_recv.at[step + 1, way, piece],
            device_id=(group, sibling),
            device_id_type=MESH,
        )

    def near_landing(step, way, piece):
        if step < 0:
            origin = sibling
        else:
            origin = device_at(-step - 1 if way == 0 else step + 1) + 1 - 2 * core
        place_of = part(o_ref.at[origin], way, piece)
        return pltpu.make_async_remote_copy(
            src_ref=place_of,
            dst_ref=place_of,
            send_sem=near_send.at[step + 1, way, piece],
            recv_sem=near_recv.at[step + 1, way, piece],
            device_id=(group, sibling),
            device_id_type=MESH,
        )

    every = [(way, piece) for piece in range(pieces) for way in range(2)]
    own = pltpu.make_async_copy(x_ref, o_ref.at[me], local_sem)

    def begin():
        barrier = pltpu.get_barrier_semaphore()
        for other in (right, left, sibling):
            pl.semaphore_signal(barrier, inc=1, device_id=(group, other), device_id_type=MESH)
        pl.semaphore_wait(barrier, 3)
        for way, piece in every:
            hop(0, way, piece).start()
        own.start()
        for way, piece in every:
            near(-1, way, piece).start()

    def stage(step):
        for way, piece in every:
            landing(step, way, piece).wait_recv()
            if step + 1 < chips - 1:
                hop(step + 1, way, piece).start()
            near(step, way, piece).start()

    def finish():
        own.wait()
        for step in range(chips - 1):
            for way, piece in every:
                hop(step, way, piece).wait_send()
        for step in range(-1, chips - 1):
            for way, piece in every:
                near(step, way, piece).wait_send()
                near_landing(step, way, piece).wait_recv()

    return begin, stage, finish


def gather_kernel(devices, pieces, x_ref, o_ref, *sems):
    begin, stage, finish = gather_moves(devices, pieces, x_ref, o_ref, *sems)
    begin()
    for step in range(devices // 2 - 1):
        stage(step)
    finish()


def gather_scratch(devices, pieces):
    dma = pltpu.SemaphoreType.DMA
    return [dma] + [dma((devices // 2, 2, pieces))] * 4


def ring_gather(x, devices, collective_id, pieces=4):
    return pl.pallas_call(
        functools.partial(gather_kernel, devices, pieces),
        out_shape=jax.ShapeDtypeStruct((devices,) + x.shape, x.dtype),
        in_specs=[pl.BlockSpec(memory_space=pltpu.HBM)],
        out_specs=pl.BlockSpec(memory_space=pltpu.HBM),
        scratch_shapes=gather_scratch(devices, pieces),
        compiler_params=pltpu.CompilerParams(collective_id=collective_id, has_side_effects=True),
    )(x)


def scatter_kernel(
    devices, pieces, x_ref, o_ref, held, near_in, ring_in, load, near_send, near_recv, send, recv
):
    chips = devices // 2
    me = lax.axis_index("shard")
    group = lax.axis_index("groups")
    core = me % 2
    place = ring_place(chips, me // 2)

    def chip_at(offset):
        return ring_chip(chips, (place + offset + 2 * chips) % chips) * 2

    right, left, sibling = chip_at(1) + core, chip_at(-1) + core, me + 1 - 2 * core
    barrier = pltpu.get_barrier_semaphore()
    for other in (right, left, sibling):
        pl.semaphore_signal(barrier, inc=1, device_id=(group, other), device_id_type=MESH)
    pl.semaphore_wait(barrier, 3)

    rows = x_ref.shape[1] // (2 * pieces)
    every = [(way, piece) for piece in range(pieces) for way in range(2)]

    def span(way, piece):
        return pl.ds((way * pieces + piece) * rows, rows)

    def target(step, way):
        return chip_at(-step - 1 if way == 0 else step + 1)

    def fetch(step, way, piece):
        return pltpu.make_async_copy(
            x_ref.at[target(step, way) + core, span(way, piece)],
            held.at[step, span(way, piece)],
            load.at[step, way, piece],
        )

    def near(step, way, piece):
        return pltpu.make_async_remote_copy(
            src_ref=x_ref.at[target(step, way) + 1 - core, span(way, piece)],
            dst_ref=near_in.at[step, span(way, piece)],
            send_sem=near_send.at[step, way, piece],
            recv_sem=near_recv.at[step, way, piece],
            device_id=(group, sibling),
            device_id_type=MESH,
        )

    def hop(step, way, piece):
        return pltpu.make_async_remote_copy(
            src_ref=held.at[step, span(way, piece)],
            dst_ref=ring_in.at[step, span(way, piece)],
            send_sem=send.at[step, way, piece],
            recv_sem=recv.at[step, way, piece],
            device_id=(group, right if way == 0 else left),
            device_id_type=MESH,
        )

    for step in range(chips):
        for way, piece in every:
            near(step, way, piece).start()
            fetch(step, way, piece).start()
    for step in range(chips):
        for way, piece in every:
            here = span(way, piece)
            fetch(step, way, piece).wait()
            near(step, way, piece).wait_recv()
            total = held[step, here, :].astype(jnp.float32) + near_in[step, here, :].astype(
                jnp.float32
            )
            if step > 0:
                hop(step - 1, way, piece).wait_recv()
                total = total + ring_in[step - 1, here, :].astype(jnp.float32)
            if step < chips - 1:
                held[step, here, :] = total.astype(held.dtype)
                hop(step, way, piece).start()
            else:
                o_ref[here, :] = total.astype(o_ref.dtype)
    for step in range(chips):
        for way, piece in every:
            near(step, way, piece).wait_send()
            if step < chips - 1:
                hop(step, way, piece).wait_send()


def ring_scatter(x, collective_id, pieces=4):
    devices, rows, depth = x.shape
    chips = devices // 2
    dma = pltpu.SemaphoreType.DMA
    sems = dma((chips, 2, pieces))
    return pl.pallas_call(
        functools.partial(scatter_kernel, devices, pieces),
        out_shape=jax.ShapeDtypeStruct((rows, depth), x.dtype),
        in_specs=[pl.BlockSpec(memory_space=pltpu.HBM)],
        out_specs=pl.BlockSpec(memory_space=pltpu.VMEM),
        scratch_shapes=[pltpu.VMEM((chips, rows, depth), x.dtype)] * 2
        + [pltpu.VMEM((chips - 1, rows, depth), x.dtype)]
        + [sems] * 5,
        compiler_params=pltpu.CompilerParams(
            collective_id=collective_id, has_side_effects=True, vmem_limit_bytes=40 << 20
        ),
    )(x)


def attend_kernel(
    devices, pieces, step_rows, heads, groups,
    count_ref, q_ref, k_ref, v_ref, w_ref, o_ref, all_ref, qs, top, total, *sems
):
    begin, stage, finish = gather_moves(devices, pieces, w_ref, all_ref, *sems)
    rows = q_ref.shape[0]
    scale = math.log2(math.e) / math.sqrt(HD)
    count = count_ref[0]
    first = lax.axis_index("shard") * rows
    blocks = (first + rows + step_rows - 1) // step_rows
    j = pl.program_id(1)
    steps = k_ref.shape[0] // step_rows
    at_step = pl.program_id(0) * steps + j
    all_steps = groups * steps

    @pl.when(at_step == 0)
    def _():
        begin()

    @pl.when(j == 0)
    def _():
        for h in range(heads):
            qs[h * rows : (h + 1) * rows, :] = q_ref[:, h * HD : (h + 1) * HD]
        top[...] = jnp.full(top.shape, NEG, jnp.float32)
        total[...] = jnp.zeros(total.shape, jnp.float32)

    def fold(masked):
        start = pl.multiple_of(j * step_rows, step_rows)
        keys = k_ref[pl.ds(start, step_rows), :]
        ones = jnp.ones((step_rows, HD), jnp.bfloat16)
        values = jnp.concatenate([v_ref[pl.ds(start, step_rows), :], ones], axis=1)
        if masked:
            at_row = first + lax.broadcasted_iota(jnp.int32, (rows, step_rows), 0)
            at_col = start + lax.broadcasted_iota(jnp.int32, (rows, step_rows), 1)
            visible = (at_col <= at_row) & (at_col < count)
        for h in range(heads):
            span = slice(h * rows, (h + 1) * rows)
            scores = lax.dot_general(
                qs[span, :], keys, (((1,), (1,)), ((), ())), preferred_element_type=jnp.float32
            )
            if masked:
                scores = jnp.where(visible, scores, NEG)
            old = top[span, :]
            new = jnp.maximum(old, jnp.max(scores, axis=1, keepdims=True) * scale)
            expo = jnp.exp2(scores * scale - new[:, :1]).astype(jnp.bfloat16)
            factor = jnp.exp2(old - new)
            part = jnp.dot(expo, values, preferred_element_type=jnp.float32)
            total[span, :] = total[span, :] * jnp.concatenate([factor, factor], axis=1) + part
            top[span, :] = new

    @pl.when(j < blocks - 1)
    def _():
        fold(False)

    @pl.when(j == blocks - 1)
    def _():
        fold(True)

        live = first + lax.broadcasted_iota(jnp.int32, (rows, HD), 0) < count
        for h in range(heads):
            both = total[h * rows : (h + 1) * rows, :]
            result = jnp.where(live, both[:, :HD] / jnp.where(live, both[:, HD:], 1.0), 0.0)
            o_ref[:, h * HD : (h + 1) * HD] = result.astype(jnp.bfloat16)

    stages = devices // 2 - 1
    for number in range(stages):

        @pl.when(at_step == (number + 1) * all_steps // stages - 1)
        def _(number=number):
            stage(number)

    @pl.when(at_step == all_steps - 1)
    def _():
        finish()


def attend(count, queries, keys_values, out_weight, kv_count, devices, collective_id, pieces=2):
    rows, width = queries.shape
    length = keys_values.shape[0]
    heads = width // HD // kv_count
    step_rows = math.gcd(length, 512)
    hbm = pl.BlockSpec(memory_space=pltpu.HBM)
    return pl.pallas_call(
        functools.partial(attend_kernel, devices, pieces, step_rows, heads, kv_count),
        grid=(kv_count, length // step_rows),
        out_shape=(
            jax.ShapeDtypeStruct((rows, width), jnp.bfloat16),
            jax.ShapeDtypeStruct((devices,) + out_weight.shape, jnp.bfloat16),
        ),
        in_specs=[
            pl.BlockSpec(memory_space=pltpu.SMEM),
            pl.BlockSpec((rows, heads * HD), lambda g, j: (0, g)),
            pl.BlockSpec((length, HD), lambda g, j: (0, g)),
            pl.BlockSpec((length, HD), lambda g, j: (0, kv_count + g)),
            hbm,
        ],
        out_specs=(pl.BlockSpec((rows, heads * HD), lambda g, j: (0, g)), hbm),
        scratch_shapes=[
            pltpu.VMEM((heads * rows, HD), jnp.bfloat16),
            pltpu.VMEM((heads * rows, HD), jnp.float32),
            pltpu.VMEM((heads * rows, 2 * HD), jnp.float32),
        ]
        + gather_scratch(devices, pieces),
        compiler_params=pltpu.CompilerParams(
            collective_id=collective_id, has_side_effects=True, vmem_limit_bytes=40 << 20
        ),
    )(count, queries, keys_values, keys_values, out_weight)


def expert_kernel(local, cap, per, count_ref, x_ref, info_ref, wg_ref, wu_ref, wd_ref, o_ref, picked, given):
    rows = x_ref.shape[1]
    start = pl.program_id(0) * per * rows
    alive = start % SEQ_LEN < count_ref[0]

    @pl.when(jnp.logical_not(alive))
    def _():
        o_ref[...] = jnp.zeros(o_ref.shape, o_ref.dtype)

    @pl.when(alive)
    def _():
        before = (
            lax.broadcasted_iota(jnp.int32, (rows, rows), 0)
            < lax.broadcasted_iota(jnp.int32, (rows, rows), 1)
        ).astype(jnp.bfloat16)
        slot_at = lax.broadcasted_iota(jnp.int32, (cap, rows), 0).astype(jnp.float32)
        choices = []
        weights = [[] for _ in range(local)]
        for b in range(per):
            info = info_ref[b]
            slots = jnp.dot(info.astype(jnp.bfloat16), before, preferred_element_type=jnp.float32)
            mine = []
            for e in range(local):
                hit = (slot_at == slots[e : e + 1]) & (info[e : e + 1] > 0.5)
                mine.append(jnp.where(hit, 1.0, 0.0))
                weights[e].append(
                    jnp.sum(
                        jnp.where(hit, info[local + e : local + e + 1], 0.0), axis=1, keepdims=True
                    )
                )
            choice = jnp.concatenate(mine, axis=0).astype(jnp.bfloat16)
            choices.append(choice)
            rows_here = jnp.dot(choice, x_ref[b], preferred_element_type=jnp.float32)
            rows_here = rows_here.astype(jnp.bfloat16)
            for e in range(local):
                picked[e, b * cap : (b + 1) * cap, :] = rows_here[e * cap : (e + 1) * cap]
        for e in range(local):
            mine = picked[e]
            gate = jnp.dot(mine, wg_ref[e], preferred_element_type=jnp.float32)
            up = jnp.dot(mine, wu_ref[e], preferred_element_type=jnp.float32)
            act = (gate / (1.0 + jnp.exp(-gate)) * up).astype(jnp.bfloat16)
            down = jnp.dot(act, wd_ref[e], preferred_element_type=jnp.float32)
            down = (down * jnp.concatenate(weights[e], axis=0)).astype(jnp.bfloat16)
            for b in range(per):
                given[b, e * cap : (e + 1) * cap, :] = down[b * cap : (b + 1) * cap]
        for b in range(per):
            back = lax.dot_general(
                choices[b], given[b], (((0,), (0,)), ((), ())), preferred_element_type=jnp.float32
            )
            o_ref[b] = back.astype(o_ref.dtype)


def expert_sums(count, rows_all, info, w_gate, w_up, w_down, cap):
    devices, rows, depth = rows_all.shape
    local, _, hidden_units = w_gate.shape
    per = 4
    whole = pl.Buffered(1)
    return pl.pallas_call(
        functools.partial(expert_kernel, local, cap, per),
        grid=(devices // per,),
        out_shape=jax.ShapeDtypeStruct((devices, rows, depth), jnp.bfloat16),
        in_specs=[
            pl.BlockSpec(memory_space=pltpu.SMEM),
            pl.BlockSpec((per, rows, depth), lambda i: (i, 0, 0)),
            pl.BlockSpec((per,) + info.shape[1:], lambda i: (i, 0, 0)),
            pl.BlockSpec(w_gate.shape, lambda i: (0, 0, 0), pipeline_mode=whole),
            pl.BlockSpec(w_up.shape, lambda i: (0, 0, 0), pipeline_mode=whole),
            pl.BlockSpec(w_down.shape, lambda i: (0, 0, 0), pipeline_mode=whole),
        ],
        out_specs=pl.BlockSpec((per, rows, depth), lambda i: (i, 0, 0)),
        scratch_shapes=[
            pltpu.VMEM((local, per * cap, depth), jnp.bfloat16),
            pltpu.VMEM((per, local * cap, depth), jnp.bfloat16),
        ],
        compiler_params=pltpu.CompilerParams(vmem_limit_bytes=60 << 20),
    )(count, rows_all, info, w_gate, w_up, w_down)


def per_device(
    hidden,
    query_rows,
    key_rows,
    value_rows,
    counts,
    out_weight,
    norm_gain,
    route_ids,
    route_weights,
    w_gate,
    w_up,
    w_down,
):
    devices = lax.axis_size("shard")
    me = lax.axis_index("shard")
    tok_dev, depth = hidden.shape
    topk = route_ids.shape[1]
    local = w_gate.shape[0]
    experts = local * devices
    capacity = max(2, tok_dev * topk * 5 // (4 * experts))
    capacity = -(-capacity // 16) * 16

    kv_width = 2 * key_rows.shape[1]
    routing = jnp.concatenate([route_ids.astype(jnp.bfloat16), route_weights], axis=1)
    routing = jnp.pad(routing, ((0, 0), (0, HD - 2 * topk)))
    both = ring_gather(jnp.concatenate([key_rows, value_rows, routing], axis=1), devices, 0)
    ids_all = both[:, :, kv_width : kv_width + topk].astype(jnp.int32)
    weights_all = both[:, :, kv_width + topk : kv_width + 2 * topk]
    live_all = jnp.arange(devices * tok_dev, dtype=jnp.int32).reshape(devices, tok_dev) < counts[0]
    info = []
    for e in range(local):
        info.append(jnp.sum((ids_all == me * local + e).astype(jnp.float32), axis=2))
    for e in range(local):
        matched = jnp.where(ids_all == me * local + e, weights_all.astype(jnp.float32), 0.0)
        info.append(jnp.where(live_all, jnp.sum(matched, axis=2), 0.0))
    info = jnp.stack(info, axis=1)
    info = jnp.pad(info, ((0, 0), (0, -info.shape[1] % 8), (0, 0)))

    both = both.reshape(devices * tok_dev, both.shape[2])
    attended, out_all = attend(
        counts, query_rows, both, out_weight, key_rows.shape[1] // HD, devices, 1
    )
    out_all = out_all.reshape(-1, depth)
    mixed_rows = hidden.astype(jnp.float32) + jnp.dot(
        attended, out_all, preferred_element_type=jnp.float32
    )
    mean_square = jnp.mean(mixed_rows * mixed_rows, axis=1, keepdims=True)
    normed = (mixed_rows * lax.rsqrt(mean_square + 1e-06) * norm_gain.astype(jnp.float32)).astype(
        jnp.bfloat16
    )
    normed_all = ring_gather(normed, devices, 2)
    sums = expert_sums(counts, normed_all, info, w_gate, w_up, w_down, capacity)
    summed = ring_scatter(sums, 3)
    return (mixed_rows + summed.astype(jnp.float32)).astype(jnp.bfloat16)


def solution(mesh):
    rows = P(("groups", "shard"), None)
    weights = P("shard", None, None)
    return jax.shard_map(
        per_device,
        mesh=mesh,
        in_specs=(
            rows,
            rows,
            rows,
            rows,
            P("groups"),
            P("shard", None),
            P(),
            rows,
            rows,
            weights,
            weights,
            weights,
        ),
        out_specs=rows,
        check_vma=False,
    )
```
